32 devices in a mesh: lag: 8 (over y, x, core), row: 4 (over z).
Axes of the slice: x: 2, y: 2, z: 4, core: 2. Of those that a mesh axis runs over, the one named last changes fastest.
Arguments:
- lag_matrix: bfloat16 [8, 8192, 8192], P('lag', 'row'), may hold values from -0.0234375 to 0.0234375
- past_current: bfloat16 [8, 256, 8192], P('lag', None, 'row'), may hold values from -6 to 6
- excitation: float32 [2, 256, 8192], P(None, None, 'row'), may hold values from -6 to 6
- block_inverse: float32 [64, 128, 128], P('row'), may hold values from -2 to 3
Outputs:
- currents: bfloat16 [2, 256, 8192], P(None, 'lag', 'row')
The draws below stay inside these ranges and needn't reach their ends.
All inputs are finite; a program needn't handle non-finite values.
Results may differ from the reference program's by a relative error of at most 0.002.
Values may be sent and summed in bfloat16 or wider, within the bound.
No kernel may reach another device: no remote copies, remote signals or barrier semaphores. Data moves between devices by JAX's collectives and lax.ppermute only.
A program may use at most 128 MiB of HBM per device.

```python
import jax
import jax.numpy as jnp
from jax import lax

N = 8192
BLOCK = 128
EXCITE = 256
STEPS = 2
LAGS = 8


def draw_block_inverse(key, part):
    inner = jax.random.fold_in(key, 11)
    shape = (N // BLOCK, BLOCK, BLOCK)
    spread = jax.random.normal(inner, shape, jnp.float32) * (0.5 / BLOCK ** 0.5)
    spread = jnp.clip(spread, -0.9, 0.9)
    return spread + jnp.eye(BLOCK, dtype=jnp.float32)[None]


def levels(own_key, extent, cuts, low, high):
    factor_of, own = 1.0, jax.random.fold_in(own_key, 6)
    for position, parts in cuts:
        draws = jnp.exp(jax.random.uniform(jax.random.fold_in(own, position), (parts,), jnp.float32, low / len(cuts), high / len(cuts)))
        factor_of = factor_of * jnp.repeat(draws, extent[position] // parts).reshape([-1 if axis == position else 1 for axis in range(len(extent))])
    return factor_of


def normal_values(own_key, dims, scale, limit, shards=(), held_as=jnp.bfloat16):
    values = scale * jax.random.normal(own_key, dims, jnp.float32)
    if shards:
        values = values * levels(own_key, dims, shards, -0.22, 0.18)
    return jnp.clip(values, -limit, limit).astype(held_as)


def setup_inputs(seed: int = 0) -> dict:
    arg_keys = jax.random.split(jax.random.key(seed), 5)
    lag_matrix = normal_values(arg_keys[0], (LAGS, N, N), (N * LAGS) ** -0.5, 0.0234375, ((0, 8), (1, 4)))
    past_current = normal_values(arg_keys[1], (LAGS, EXCITE, N), 1.0, 6.0, ((0, 8), (2, 4)))
    excitation = normal_values(arg_keys[2], (STEPS, EXCITE, N), 1.0, 6.0, ((2, 4),), jnp.float32)
    block_inverse = draw_block_inverse(jax.random.fold_in(arg_keys[4], 71), 0)
    return dict(lag_matrix=lag_matrix, past_current=past_current, excitation=excitation, block_inverse=block_inverse)


def solve_blocks(source, block_inverse):
    pieces = source.reshape(EXCITE, N // BLOCK, BLOCK)
    result = jnp.einsum("bij,rbj->rbi", block_inverse, pieces, precision=lax.Precision.HIGHEST)
    return result.reshape(EXCITE, N).astype(jnp.bfloat16)


def reference(lag_matrix, past_current, excitation, block_inverse):
    history_cur = past_current
    results = []
    for step in range(STEPS):
        def add_lag(total, pair):
            matrix, current = pair
            return total + jnp.dot(current, matrix.T, preferred_element_type=jnp.float32), None

        history, _ = lax.scan(add_lag, jnp.zeros((EXCITE, N), jnp.float32), (lag_matrix, history_cur))
        source = excitation[step] - history
        newest = solve_blocks(source, block_inverse)
        results.append(newest)
        history_cur = jnp.concatenate([newest[None], history_cur[:-1]], axis=0)
    return jnp.stack(results)
```

```python
import jax
import jax.numpy as jnp
from jax import lax
from jax.sharding import PartitionSpec as P

CHUNKS = 1


def contract(x, matrix, block, total=None):
    width = x.shape[1]
    part = lax.dynamic_slice_in_dim(matrix, block * width, width, 1)
    value = lax.dot_general(
        x, part, (((1,), (1,)), ((), ())), preferred_element_type=jnp.float32
    )
    return value if total is None else total + value


def solve_blocks(source, inverse):
    count = source.shape[0]
    pieces = source.reshape(count, inverse.shape[0], inverse.shape[1])
    result = jnp.einsum("bij,rbj->rbi", inverse, pieces, precision=lax.Precision.HIGHEST)
    return result.reshape(count, source.shape[1]).astype(jnp.bfloat16)


def line_slots(x, row, rows):
    slots = [(x, row, list(range(rows)))]
    left = right = x
    for step in range(1, rows):
        up = list(range(step - 1, rows - 1))
        down = list(range(1, rows - step + 1))
        from_left = [i + 1 for i in up]
        from_right = [i - 1 for i in down]
        up_pairs = [(i, i + 1) for i in up]
        down_pairs = [(i, i - 1) for i in down]
        if set(up) & set(down):
            left = lax.ppermute(left, "row", up_pairs)
            right = lax.ppermute(right, "row", down_pairs)
            if set(from_left) & set(from_right):
                slots.append((left, jnp.maximum(row - step, 0), from_left))
                slots.append((right, jnp.minimum(row + step, rows - 1), from_right))
                continue
            left = right = jnp.where(row >= step, left, right)
        else:
            left = right = lax.ppermute(left, "row", up_pairs + down_pairs)
        block = jnp.where(row >= step, row - step, jnp.minimum(row + step, rows - 1))
        slots.append((left, block, from_left + from_right))
    return slots


def per_device(lag_matrix, past_current, excitation, block_inverse):
    lags, rows = lax.axis_size("lag"), lax.axis_size("row")
    lag, row = lax.axis_index("lag"), lax.axis_index("row")
    chips, chip, core = lags // 2, lag // 2, lag % 2
    matrix = lag_matrix[0]
    own = past_current[0]
    excite, width = own.shape
    half = width // 2
    blocks = block_inverse.shape[0] // 2
    share = excite // chips
    part = share // CHUNKS
    inverse = lax.dynamic_slice_in_dim(block_inverse, core * blocks, blocks, 0)
    drive = lax.dynamic_slice(
        excitation, (0, chip * share, core * half), (excitation.shape[0], share, half)
    ).reshape(excitation.shape[0], CHUNKS, part, half)
    split = own.reshape(chips, CHUNKS, part, width)

    def older(value, senders):
        pairs = [
            (k * rows + i, (k + 1) * rows + i) for k in range(lags - 1) for i in senders
        ]
        return lax.ppermute(value, ("lag", "row"), pairs)

    def reduce_lags(value):
        mine = lax.dynamic_slice_in_dim(value, core * half, half, 1)
        other = lax.dynamic_slice_in_dim(value, (1 - core) * half, half, 1)
        pair = mine + lax.ppermute(other, "lag", [(i, i ^ 1) for i in range(lags)])
        pair = pair.reshape(chips, part, half)
        total = lax.dynamic_index_in_dim(pair, chip, 0, keepdims=False)
        for d in range(1, chips):
            sent = lax.dynamic_index_in_dim(pair, chip ^ d, 0, keepdims=False)
            total += lax.ppermute(sent, "lag", [(i, i ^ (2 * d)) for i in range(lags)])
        return total

    results = []
    for c in range(CHUNKS):
        x = split[:, c].reshape(chips * part, width)
        first = second = None
        for value, block, senders in line_slots(x, row, rows):
            first = contract(value, matrix, block, first)
            second = contract(older(value, senders), matrix, block, second)
        news = solve_blocks(drive[0, c] - reduce_lags(first), inverse)
        rest = reduce_lags(second)

        last = None
        for d in range(rows):
            there = lax.ppermute(news, "row", [(i, i ^ d) for i in range(rows)]) if d else news
            pieces = [there]
            for k in range(1, chips):
                pieces.append(lax.ppermute(there, "lag", [(2 * k, 0), (2 * k + 1, 1)]))
            joined = jnp.concatenate(pieces, axis=0)
            beside = lax.ppermute(joined, "lag", [(1, 0)])
            last = contract(jnp.concatenate([joined, beside], axis=1), matrix, row ^ d, last)
        last = last.reshape(chips, part, width)
        mine = last[0, :, :half]
        other = last[:, :, half:]
        other = lax.ppermute(other, "lag", [(0, 1)])
        mine = jnp.where(core == 0, last[:, :, :half], other)
        term = mine[0]
        for k in range(1, chips):
            term = jnp.where(
                chip == k, lax.ppermute(mine[k], "lag", [(0, 2 * k), (1, 2 * k + 1)]), term
            )
        finals = solve_blocks(drive[1, c] - rest - term, inverse)
        results.append((news, finals))

    both = jnp.stack(
        [jnp.concatenate([r[s] for r in results], axis=0) for s in range(2)]
    )
    rows_each = share // 2
    keep = lax.dynamic_slice_in_dim(both, core * rows_each, rows_each, 1)
    give = lax.dynamic_slice_in_dim(both, (1 - core) * rows_each, rows_each, 1)
    got = lax.ppermute(give, "lag", [(i, i ^ 1) for i in range(lags)])
    low = jnp.where(core == 0, keep, got)
    high = jnp.where(core == 0, got, keep)
    return jnp.concatenate([low, high], axis=2)


def solution(mesh):
    in_specs = (
        P("lag", "row", None),
        P("lag", None, "row"),
        P(None, None, "row"),
        P("row", None, None),
    )
    out_specs = P(None, "lag", "row")
    return jax.shard_map(
        per_device, mesh=mesh, in_specs=in_specs, out_specs=out_specs, check_vma=False
    )
```

```python
import functools

import jax
import jax.numpy as jnp
from jax import lax
from jax.experimental import pallas as pl
from jax.experimental.pallas import tpu as pltpu
from jax.sharding import PartitionSpec as P

PIECES = 2


def product_kernel(idx, *refs, count, groups, add):
    xs, a_ref = refs[:count], refs[count]
    rest = list(refs[count + 1 :])
    c_refs = [rest.pop(0) for _ in range(groups)] if add else None
    o_refs = [rest.pop(0) for _ in range(groups)]
    buf = xs[0]
    if count > 1:
        buf = rest.pop(0)

        @pl.when(pl.program_id(0) == 0)
        def _():
            at = 0
            for x in xs:
                buf[at : at + x.shape[0]] = x[...]
                at += x.shape[0]

    def put(values):
        at = 0
        for k, o in enumerate(o_refs):
            rows = o.shape[1]
            if values is None:
                o[0] = c_refs[k][0]
            elif add:
                o[0] = c_refs[k][0] + values[at : at + rows]
            else:
                o[0] = values[at : at + rows]
            at += rows

    def value():
        return lax.dot_general(
            buf[...], a_ref[...], (((1,), (1,)), ((), ())), preferred_element_type=jnp.float32
        )

    if not add:
        put(value())
        return

    @pl.when(idx[2] != 0)
    def _():
        put(value())

    @pl.when(idx[2] == 0)
    def _():
        put(None)


def product(idx, xs, matrix, totals=None, side=None, groups=1):
    count, width = len(xs), xs[0].shape[1]
    rows = sum(x.shape[0] for x in xs)
    each = rows // groups
    half = matrix.shape[0] // 2
    first, steps = (0, 2) if side is None else (side, 1)
    in_specs = [pl.BlockSpec(x.shape, lambda t, s: (0, 0)) for x in xs]
    in_specs.append(pl.BlockSpec((half, width), lambda t, s: ((1 - s[1] + t + first) % 2, s[0])))
    operands = [*xs, matrix]
    if totals is not None:
        in_specs += [pl.BlockSpec((1, each, half), lambda t, s: (t + first, 0, 0))] * groups
        operands += totals
    scratch = [pltpu.VMEM((rows, width), xs[0].dtype)] if count > 1 else []
    return pl.pallas_call(
        functools.partial(product_kernel, count=count, groups=groups, add=totals is not None),
        out_shape=[jax.ShapeDtypeStruct((steps, each, half), jnp.float32)] * groups,
        grid_spec=pltpu.PrefetchScalarGridSpec(
            num_scalar_prefetch=1,
            grid=(steps,),
            in_specs=in_specs,
            out_specs=[pl.BlockSpec((1, each, half), lambda t, s: (t, 0, 0))] * groups,
            scratch_shapes=scratch,
        ),
        compiler_params=pltpu.CompilerParams(
            dimension_semantics=("arbitrary",), vmem_limit_bytes=36 << 20
        ),
        cost_estimate=pl.CostEstimate(
            flops=2 * rows * steps * half * width,
            bytes_accessed=steps * half * (2 * width + 8 * rows),
            transcendentals=0,
        ),
    )(idx, *operands)


def solve_blocks(source, inverse):
    count = source.shape[0]
    pieces = source.reshape(count, inverse.shape[0], inverse.shape[1])
    result = jnp.einsum("bij,rbj->rbi", inverse, pieces, precision=lax.Precision.HIGHEST)
    return result.reshape(count, source.shape[1]).astype(jnp.bfloat16)


def line_slots(x, row, rows):
    cut = x.shape[0] // PIECES
    left = right = [x[k * cut : (k + 1) * cut] for k in range(PIECES)]
    yield [x], row, row >= 0, list(range(rows))

    def send(pieces, pairs):
        out = []
        for piece in pieces:
            out.append(lax.ppermute(piece, "row", pairs))
        return out

    for step in range(1, rows):
        up = list(range(step - 1, rows - 1))
        down = list(range(1, rows - step + 1))
        from_left = [i + 1 for i in up]
        from_right = [i - 1 for i in down]
        up_pairs = [(i, i + 1) for i in up]
        down_pairs = [(i, i - 1) for i in down]
        if set(up) & set(down):
            left = send(left, up_pairs)
            right = send(right, down_pairs)
            if set(from_left) & set(from_right):
                yield left, jnp.maximum(row - step, 0), row >= step, from_left
                yield right, jnp.minimum(row + step, rows - 1), row + step < rows, from_right
                continue
            left = right = [jnp.where(row >= step, a, b) for a, b in zip(left, right)]
        else:
            left = right = send(left, up_pairs + down_pairs)
        block = jnp.where(row >= step, row - step, jnp.minimum(row + step, rows - 1))
        yield left, block, (row >= step) | (row + step < rows), from_left + from_right


def per_device(lag_matrix, past_current, excitation, block_inverse):
    lags, rows = lax.axis_size("lag"), lax.axis_size("row")
    lag, row = lax.axis_index("lag"), lax.axis_index("row")
    chips, chip, core = lags // 2, lag // 2, lag % 2
    matrix = lag_matrix[0]
    own = past_current[0]
    excite, width = own.shape
    half = width // 2
    blocks = block_inverse.shape[0] // 2
    share = excite // chips
    inverse = lax.dynamic_slice_in_dim(block_inverse, core * blocks, blocks, 0)
    drive = lax.dynamic_slice(
        excitation, (0, chip * share, core * half), (excitation.shape[0], share, half)
    )
    mate = [(i, i ^ 1) for i in range(lags)]

    def index(block, flag):
        return jnp.stack([block, core, flag.astype(jnp.int32)])

    def older(value, senders):
        pairs = [
            (k * rows + i, (k + 1) * rows + i) for k in range(lags - 1) for i in senders
        ]
        return lax.ppermute(value, ("lag", "row"), pairs)

    def halves(xs, idx, total):
        (other,) = product(idx, xs, matrix, total, 0)
        got = lax.ppermute(other, "lag", mate)
        (mine,) = product(idx, xs, matrix, total, 1)
        return mine + got

    def reduce_chips(pair):
        pair = pair.reshape(chips, share, half)
        total = lax.dynamic_index_in_dim(pair, chip, 0, keepdims=False)
        for d in range(1, chips):
            sent = lax.dynamic_index_in_dim(pair, chip ^ d, 0, keepdims=False)
            total += lax.ppermute(sent, "lag", [(i, i ^ (2 * d)) for i in range(lags)])
        return total

    total = None
    slots = list(line_slots(own, row, rows))
    for pieces, block, valid, senders in slots[:-1]:
        value = pieces[0] if len(pieces) == 1 else jnp.concatenate(pieces, axis=0)
        total = product(
            index(block, valid), [value, older(value, senders)], matrix, total, groups=2
        )
    pieces, block, valid, senders = slots[-1]
    idx = index(block, valid)
    pair = halves(pieces, idx, total[:1])
    news = solve_blocks(drive[0] - reduce_chips(pair), inverse)
    late = [older(piece, senders) for piece in pieces]
    second = product(idx, late, matrix, total[1:])

    beside = lax.ppermute(news, "lag", mate)
    whole = jnp.concatenate(
        [jnp.where(core == 0, news, beside), jnp.where(core == 0, beside, news)], axis=1
    )
    far = [k for k in range(1, chips) if k & (k - 1)]
    near = [k for k in range(1, chips) if not k & (k - 1)]

    def to_first(x, k):
        return lax.ppermute(x, "lag", [(2 * k, 0)])

    def along(x, d, which):
        pairs = [(k * rows + i, k * rows + (i ^ d)) for k in which for i in range(rows)]
        return lax.ppermute(x, ("lag", "row"), pairs)

    near_here = [to_first(whole, k) for k in near]
    far_here = [to_first(whole, k) for k in far]
    away = [along(whole, d, [2 * k for k in [0] + near]) for d in range(1, rows)]
    far_stack = jnp.concatenate(far_here, axis=0)
    far_away = [far_stack] + [along(far_stack, d, [0]) for d in range(1, rows)]
    near_away = [[to_first(away[d - 1], k) for k in near] for d in range(1, rows)]
    first = lag == 0
    order = [0] + far + near
    for d in range(rows):
        if d == 0:
            one, close = whole, near_here
        else:
            one = away[d - 1]
            close = near_away[d - 1]
        fars = [far_away[d][j * share : (j + 1) * share] for j in range(len(far))]
        parts = [one] + fars + close
        parts = [parts[order.index(k)] for k in range(chips)]
        idx = index(row ^ d, first)
        if d < rows - 1:
            second = product(idx, parts, matrix, second)
        else:
            pair = halves(parts, idx, second)
    finals = solve_blocks(drive[1] - reduce_chips(pair), inverse)
    beside = lax.ppermute(finals, "lag", mate)
    final = jnp.concatenate(
        [jnp.where(core == 0, finals, beside), jnp.where(core == 0, beside, finals)], axis=1
    )
    count = share // 2
    return jnp.stack(
        [lax.dynamic_slice_in_dim(x, core * count, count, 0) for x in (whole, final)]
    )


def solution(mesh):
    in_specs = (
        P("lag", "row", None),
        P("lag", None, "row"),
        P(None, None, "row"),
        P("row", None, None),
    )
    out_specs = P(None, "lag", "row")

    return jax.shard_map(
        per_device, mesh=mesh, in_specs=in_specs, out_specs=out_specs, check_vma=False
    )
```

```python
import functools

import jax
import jax.numpy as jnp
from jax import lax
from jax.experimental import pallas as pl
from jax.experimental.pallas import tpu as pltpu
from jax.sharding import PartitionSpec as P


def product_kernel(idx, *refs, count, groups, add, shared):
    xs, a_ref = refs[:count], refs[count]
    rest = list(refs[count + 1 :])
    b_ref = rest.pop(0) if shared else None
    c_refs = [rest.pop(0) for _ in range(groups)] if add else None
    o_refs = [rest.pop(0) for _ in range(groups)]
    buf = xs[0]
    if count > 1:
        buf = rest.pop(0)

        @pl.when(pl.program_id(0) == 0)
        def _():
            at = 0
            for x in xs:
                buf[at : at + x.shape[0]] = x[...]
                at += x.shape[0]

    def put(values):
        at = 0
        for k, o in enumerate(o_refs):
            rows = o.shape[1]
            if values is None:
                o[0] = c_refs[k][0]
            elif add:
                o[0] = c_refs[k][0] + values[at : at + rows]
            else:
                o[0] = values[at : at + rows]
            at += rows

    def value(ref):
        return lax.dot_general(
            buf[...], ref[...], (((1,), (1,)), ((), ())), preferred_element_type=jnp.float32
        )

    if not add:
        put(value(a_ref))
        return

    @pl.when(idx[2] == 1)
    def _():
        put(value(a_ref))

    if shared:

        @pl.when(idx[2] == 2)
        def _():
            put(value(b_ref))

    @pl.when(idx[2] == 0)
    def _():
        put(None)


def product(idx, xs, matrix, totals=None, side=None, groups=1, mates=None):
    places = [x if isinstance(x, tuple) else (x, None) for x in xs]
    count, width = len(xs), places[0][0].shape[-1]
    rows = sum(x.shape[-2] for x, _ in places)
    each = rows // groups
    half = matrix.shape[0] // 2
    first, steps = (0, 2) if side is None else (side, 1)
    in_specs, stacked = [], []
    for x, place in places:
        stacked.append(x)
        if place is None:
            in_specs.append(pl.BlockSpec(x.shape, lambda t, s: (0, 0)))
        else:
            in_specs.append(
                pl.BlockSpec((None, *x.shape[1:]), lambda t, s, place=place: (place, 0, 0))
            )
    tile = lambda t, s: (1 - s[1] + t + first) % 2
    operands = [*stacked, matrix]
    if mates is None:
        in_specs.append(pl.BlockSpec((half, width), lambda t, s: (tile(t, s), s[0])))
    else:
        keep = lambda want, s, x: jnp.where(s[2] == want, x, 0)
        in_specs.append(
            pl.BlockSpec((half, width), lambda t, s: (keep(1, s, tile(t, s)), keep(1, s, s[0])))
        )
        in_specs.append(
            pl.BlockSpec(
                (None, half, width), lambda t, s: (keep(2, s, s[3]), keep(2, s, tile(t, s)), 0)
            )
        )
        operands.append(mates)
    if totals is not None:
        in_specs += [pl.BlockSpec((1, each, half), lambda t, s: (t + first, 0, 0))] * groups
        operands += totals
    scratch = [pltpu.VMEM((rows, width), matrix.dtype)] if count > 1 else []
    return pl.pallas_call(
        functools.partial(
            product_kernel,
            count=count,
            groups=groups,
            add=totals is not None,
            shared=mates is not None,
        ),
        out_shape=[jax.ShapeDtypeStruct((steps, each, half), jnp.float32)] * groups,
        grid_spec=pltpu.PrefetchScalarGridSpec(
            num_scalar_prefetch=1,
            grid=(steps,),
            in_specs=in_specs,
            out_specs=[pl.BlockSpec((1, each, half), lambda t, s: (t, 0, 0))] * groups,
            scratch_shapes=scratch,
        ),
        compiler_params=pltpu.CompilerParams(
            dimension_semantics=("arbitrary",), vmem_limit_bytes=(32 if groups > 1 else 24) << 20
        ),
        cost_estimate=pl.CostEstimate(
            flops=2 * rows * steps * half * width,
            bytes_accessed=steps * half * (2 * width + 8 * rows),
            transcendentals=0,
        ),
    )(idx, *operands)


def copy_kernel(x_ref, o_ref):
    o_ref[0] = x_ref[...]


def second_halves(matrix, blocks):
    rows, half = matrix.shape[0], matrix.shape[1] // blocks // 2
    return pl.pallas_call(
        copy_kernel,
        out_shape=jax.ShapeDtypeStruct((blocks, rows, half), matrix.dtype),
        grid=(blocks, 2),
        in_specs=[pl.BlockSpec((rows // 2, half), lambda b, t: (t, 2 * b + 1))],
        out_specs=pl.BlockSpec((1, rows // 2, half), lambda b, t: (b, t, 0)),
        compiler_params=pltpu.CompilerParams(
            dimension_semantics=("arbitrary", "arbitrary"), vmem_limit_bytes=24 << 20
        ),
        cost_estimate=pl.CostEstimate(
            flops=0, bytes_accessed=4 * blocks * rows * half, transcendentals=0
        ),
        name="cp",
    )(matrix)


def solve_blocks(source, inverse):
    count = source.shape[0]
    pieces = source.reshape(count, inverse.shape[0], inverse.shape[1])
    result = jnp.einsum("bij,rbj->rbi", inverse, pieces, precision=lax.Precision.HIGHEST)
    return result.reshape(count, source.shape[1]).astype(jnp.bfloat16)


def line_slots(x, row, rows):
    left = right = x
    yield x, row, row >= 0, list(range(rows))

    def send(value, pairs):
        return lax.ppermute(value, "row", pairs)

    for step in range(1, rows):
        up = list(range(step - 1, rows - 1))
        down = list(range(1, rows - step + 1))
        from_left = [i + 1 for i in up]
        from_right = [i - 1 for i in down]
        up_pairs = [(i, i + 1) for i in up]
        down_pairs = [(i, i - 1) for i in down]
        if set(up) & set(down):
            left = send(left, up_pairs)
            right = send(right, down_pairs)
            if set(from_left) & set(from_right):
                yield left, jnp.maximum(row - step, 0), row >= step, from_left
                yield right, jnp.minimum(row + step, rows - 1), row + step < rows, from_right
                continue
            left = right = jnp.where(row >= step, left, right)
        else:
            left = right = send(left, up_pairs + down_pairs)
        block = jnp.where(row >= step, row - step, jnp.minimum(row + step, rows - 1))
        yield left, block, (row >= step) | (row + step < rows), from_left + from_right


def per_device(lag_matrix, past_current, excitation, block_inverse):
    lags, rows = lax.axis_size("lag"), lax.axis_size("row")
    lag, row = lax.axis_index("lag"), lax.axis_index("row")
    chips, chip, core = lags // 2, lag // 2, lag % 2
    matrix = lag_matrix[0]
    own = past_current[0]
    excite, width = own.shape
    half = width // 2
    blocks = block_inverse.shape[0] // 2
    share = excite // chips
    inverse = lax.dynamic_slice_in_dim(block_inverse, core * blocks, blocks, 0)
    drive = lax.dynamic_slice(
        excitation, (0, chip * share, core * half), (excitation.shape[0], share, half)
    )
    mate = [(i, i ^ 1) for i in range(lags)]

    def index(block, flag):
        return jnp.stack([block, core, flag.astype(jnp.int32), row * 0])

    def older(value, senders):
        pairs = [
            (k * rows + i, (k + 1) * rows + i) for k in range(lags - 1) for i in senders
        ]
        return lax.ppermute(value, ("lag", "row"), pairs)

    def halves(xs, idx, total, mates=None):
        (other,) = product(idx, xs, matrix, total, 0, mates=mates)
        got = lax.ppermute(other, "lag", mate)
        (mine,) = product(idx, xs, matrix, total, 1, mates=mates)
        return mine.reshape(chips, share, half), got.reshape(chips, share, half)

    def reduce_chips(mine, got):
        pick = lambda k: lax.dynamic_index_in_dim(
            mine, k, 0, keepdims=False
        ) + lax.dynamic_index_in_dim(got, k, 0, keepdims=False)
        total = pick(chip)
        for d in range(1, chips):
            total += lax.ppermute(pick(chip ^ d), "lag", [(i, i ^ (2 * d)) for i in range(lags)])
        return total

    seconds = second_halves(matrix, rows)
    mates = lax.ppermute(seconds, "lag", mate)

    total = None
    slots = list(line_slots(own, row, rows))
    for value, block, valid, senders in slots[:-1]:
        total = product(
            index(block, valid), [value, older(value, senders)], matrix, total, groups=2
        )
    value, block, valid, senders = slots[-1]
    late = index(block, valid)
    news = solve_blocks(drive[0] - reduce_chips(*halves([value], late, total[:1])), inverse)
    last = older(value, senders)

    far = [k for k in range(1, chips) if k & (k - 1)]
    near = [k for k in range(1, chips) if not k & (k - 1)]

    def to_first(x, k):
        return lax.ppermute(x, "lag", [(2 * k, 0), (2 * k + 1, 1)])

    def along(x, d, which):
        pairs = [
            ((2 * k + c) * rows + i, (2 * k + c) * rows + (i ^ d))
            for k in which
            for c in range(2)
            for i in range(rows)
        ]
        return lax.ppermute(x, ("lag", "row"), pairs)

    near_here = [to_first(news, k) for k in near]
    far_here = jnp.concatenate([to_first(news, k) for k in far], axis=0)
    away = [along(news, d, [0] + near) for d in range(1, rows)]
    far_away = [far_here] + [along(far_here, d, [0]) for d in range(1, rows)]
    stack = jnp.stack(away)
    near_away = [to_first(stack, k) for k in near]
    which = jnp.where(chip == 0, 1 + core, 0)
    order = [0] + far + near
    second = total[1:]
    for d in range(rows):
        one, close = (news, near_here) if d == 0 else (away[d - 1], [(x, d - 1) for x in near_away])
        fars = [far_away[d][j * share : (j + 1) * share] for j in range(len(far))]
        parts = [one] + fars + close
        parts = [parts[order.index(k)] for k in range(chips)]
        block = row ^ d
        idx = jnp.stack([2 * block, core, which, block])
        if d < rows - 1:
            second = product(idx, parts, matrix, second, mates=mates)
        else:
            pair = halves(parts, idx, second, mates)
        if d == 0:
            second = product(late, [last], matrix, second)
    finals = solve_blocks(drive[1] - reduce_chips(*pair), inverse)

    def assemble(x):
        count = share // 2
        keep = lax.dynamic_slice_in_dim(x, core * count, count, 0)
        give = lax.dynamic_slice_in_dim(x, (1 - core) * count, count, 0)
        got = lax.ppermute(give, "lag", mate)
        return jnp.concatenate(
            [jnp.where(core == 0, keep, got), jnp.where(core == 0, got, keep)], axis=1
        )

    return jnp.stack([assemble(news), assemble(finals)])


def solution(mesh):
    in_specs = (
        P("lag", "row", None),
        P("lag", None, "row"),
        P(None, None, "row"),
        P("row", None, None),
    )
    out_specs = P(None, "lag", "row")

    return jax.shard_map(
        per_device, mesh=mesh, in_specs=in_specs, out_specs=out_specs, check_vma=False
    )
```
